32 devices in a mesh: dp: 4 (over y, core), seq: 8 (over z, x).
Axes of the slice: x: 2, y: 2, z: 4, core: 2. Of those that a mesh axis runs over, the one named last changes fastest.
Arguments:
- layer_input: bfloat16 [2, 4, 1024, 768], P(None, 'dp', 'seq'), may hold values from -6 to 6
- cotangent: bfloat16 [2, 4, 1024, 768], P(None, 'dp', 'seq'), may hold values from -6 to 6
- w_joined: bfloat16 [768, 2304], P(('dp', 'seq')), may hold values from -3 to 3
- w_output: bfloat16 [768, 768], P(('dp', 'seq')), may hold values from -2.5 to 2.5
- w_expand: bfloat16 [768, 2304], P(('dp', 'seq')), may hold values from -0.21875 to 0.21875
- w_contract: bfloat16 [1152, 768], P(None, ('dp', 'seq')), may hold values from -0.1875 to 0.1875
- gain_one: bfloat16 [768], P(('dp', 'seq')), may hold values from 0.5 to 1.5
- gain_two: bfloat16 [768], P(('dp', 'seq')), may hold values from 0.5 to 1.5
Outputs:
- layer_output: bfloat16 [2, 4, 1024, 768], P(None, 'dp', 'seq')
- input_grad: bfloat16 [2, 4, 1024, 768], P(None, 'dp', 'seq')
- w_joined_grad: float32 [768, 2304], P(('dp', 'seq'))
- w_output_grad: float32 [768, 768], P(('dp', 'seq'))
- w_expand_grad: float32 [768, 2304], P(('dp', 'seq'))
- w_contract_grad: float32 [1152, 768], P(None, ('dp', 'seq'))
- gain_one_grad: float32 [768], P(('dp', 'seq'))
- gain_two_grad: float32 [768], P(('dp', 'seq'))
The draws below stay inside these ranges and needn't reach their ends.
All inputs are finite; a program needn't handle non-finite values.
Results may differ from the reference program's by a relative error of at most 0.02.
The reference program's roundings to bfloat16 on the way (of `normed_one`, `attended`, `normed_two`, `mixed`, `d_expanded`, `d_attended`, `d_scores` and `d_joined`) count: a program that leaves them out, or rounds other values in their place, can miss the bound.
Values may be sent and summed in bfloat16 or wider, within the bound.
A program may use at most 128 MiB of HBM per device.

```python
import math
import jax
import jax.numpy as jnp
from jax import lax

D = 768
HEADS = 12
HEAD_DIM = 64
FF = 1152
WINDOW = 128
MB = 2
BATCH = 4
LENGTH = 1024


def draw_w_joined(key, part):
    base = jax.random.truncated_normal(jax.random.fold_in(key, 11), -4.0, 4.0, (D, 3 * D), jnp.float32) / math.sqrt(D)
    return base.astype(jnp.bfloat16)


def block_levels(key, dims, pieces, smallest, top_value):
    level = 1.0
    for dim, shards_of in pieces:
        steps = jax.random.uniform(jax.random.fold_in(jax.random.fold_in(key, 6), dim), (shards_of,), jnp.float32, smallest / len(pieces), top_value / len(pieces))
        level = level * jnp.repeat(jnp.exp(steps), dims[dim] // shards_of).reshape((-1,) + (1,) * (len(dims) - 1 - dim))
    return level


def scatter_about(key, dims, deviation, bound, pieces=(), kind=jnp.bfloat16):
    level = block_levels(key, dims, pieces, -0.22, 0.18) if pieces else 1.0
    entries = jax.random.normal(key, dims, jnp.float32) * deviation * level
    return jnp.minimum(jnp.maximum(entries, -bound), bound).astype(kind)


def setup_inputs(seed: int = 0) -> dict:
    splits = jax.random.split(jax.random.key(seed), 9)
    layer_input = scatter_about(splits[0], (MB, BATCH, LENGTH, D), 1.0, 6.0, ((1, 4), (2, 8)))
    cotangent = scatter_about(splits[1], (MB, BATCH, LENGTH, D), 1.0, 6.0, ((1, 4), (2, 8)))
    w_joined = draw_w_joined(jax.random.fold_in(splits[8], 71), 0)
    w_output = scatter_about(splits[3], (D, D), (D // 128) ** -0.5, 2.5, ((0, 32),))
    w_expand = scatter_about(splits[4], (D, 2 * FF), D ** -0.5, 0.21875, ((0, 32),))
    w_contract = scatter_about(splits[5], (FF, D), FF ** -0.5, 0.1875, ((1, 32),))
    gain_one = jnp.clip(1.0 + 0.1 * jax.random.normal(splits[6], (D,), jnp.float32), 0.5, 1.5).astype(jnp.bfloat16)
    gain_two = jnp.clip(1.0 + 0.1 * jax.random.normal(splits[7], (D,), jnp.float32), 0.5, 1.5).astype(jnp.bfloat16)
    return dict(layer_input=layer_input, cotangent=cotangent, w_joined=w_joined, w_output=w_output, w_expand=w_expand, w_contract=w_contract, gain_one=gain_one, gain_two=gain_two)


NORM_EPS = 1e-05
ROPE_BASE = 10000.0
MASK_FILL = -1e+30
SQRT_HALF = 0.7071067811865476
INV_ROOT_TAU = 0.3989422804014327

def norm_apply(values, gain):
    center = lax.optimization_barrier(jnp.mean(values, axis=-1, keepdims=True))
    shifted = values - center
    inv_std = lax.rsqrt(lax.optimization_barrier(jnp.mean(shifted * shifted, axis=-1, keepdims=True)) + NORM_EPS)
    normed = shifted * inv_std
    return (normed * gain.astype(jnp.float32), normed, inv_std)

def norm_back(upstream, normed, inv_std, gain):
    scaled = upstream * gain.astype(jnp.float32)
    inner = scaled - lax.optimization_barrier(jnp.mean(scaled, axis=-1, keepdims=True)) - normed * lax.optimization_barrier(jnp.mean(scaled * normed, axis=-1, keepdims=True))
    return (inv_std * inner, lax.optimization_barrier(jnp.sum(upstream * normed, axis=0)))

def gelu_slope(values):
    cumul = 0.5 * (1.0 + jax.scipy.special.erf(values * SQRT_HALF))
    return cumul + values * jnp.exp(-0.5 * values * values) * INV_ROOT_TAU

def rope_tables(positions, head_dim):
    half_dim = head_dim // 2
    freqs = ROPE_BASE ** (-jnp.arange(half_dim).astype(jnp.float32) * 2.0 / head_dim)
    angles = positions.astype(jnp.float32)[:, None] * freqs[None, :]
    return (jnp.cos(angles)[:, None, :], jnp.sin(angles)[:, None, :])

def rotate(values, cosine, sine):
    half_dim = values.shape[-1] // 2
    first = values[..., :half_dim]
    second = values[..., half_dim:]
    return jnp.concatenate([first * cosine - second * sine, second * cosine + first * sine], axis=-1)

def unrotate(values, cosine, sine):
    half_dim = values.shape[-1] // 2
    first = values[..., :half_dim]
    second = values[..., half_dim:]
    return jnp.concatenate([first * cosine + second * sine, second * cosine - first * sine], axis=-1)

def block_scores(block_index, q_rot, key_pad, qblock, half):
    start = block_index * qblock
    query_blk = lax.dynamic_slice_in_dim(q_rot, start, qblock, 0).astype(jnp.float32)
    key_blk = lax.dynamic_slice_in_dim(key_pad, start, qblock + 2 * half, 0).astype(jnp.float32)
    scores = jnp.einsum('qhd,khd->hqk', query_blk, key_blk) * q_rot.shape[-1] ** (-0.5)
    query_pos = start + jnp.arange(qblock, dtype=jnp.int32)[:, None]
    key_pos = start - half + jnp.arange(qblock + 2 * half, dtype=jnp.int32)[None, :]
    allowed = (jnp.abs(query_pos - key_pos) <= half) & (key_pos >= 0) & (key_pos < LENGTH)
    return (jnp.where(allowed[None], scores, MASK_FILL), query_blk, key_blk)

def spread_keys(blocks, half, qblock):
    count = blocks.shape[0]
    rest = blocks.shape[2:]
    extra = [(0, 0)] * len(rest)
    main_rows = blocks[:, :qblock].reshape((count * qblock,) + rest)
    tails = jnp.pad(blocks[:, qblock:], [(0, 0), (0, qblock - 2 * half)] + extra).reshape((count * qblock,) + rest)
    total = jnp.pad(main_rows, [(0, 2 * half)] + extra) + jnp.pad(tails, [(qblock, 0)] + extra)[:count * qblock + 2 * half]
    return total[half:half + count * qblock]

def one_sequence(source, upstream_half, weights):
    w_joined, w_output, w_expand, w_contract, gain_one, gain_two = weights
    half = WINDOW // 2
    qblock = min(512, LENGTH)
    blocks_count = LENGTH // qblock
    heads, head_dim = (HEADS, HEAD_DIM)
    width = D
    source32 = source.astype(jnp.float32)
    upstream = upstream_half.astype(jnp.float32)
    normed_f, norm_one, inv_one = norm_apply(source32, gain_one)
    normed_one = normed_f.astype(jnp.bfloat16)
    joined = jnp.dot(normed_one, w_joined, preferred_element_type=jnp.float32)
    cosine, sine = rope_tables(jnp.arange(LENGTH, dtype=jnp.int32), head_dim)
    q_rot = rotate(joined[:, :width].reshape(LENGTH, heads, head_dim), cosine, sine).astype(jnp.bfloat16)
    k_rot = rotate(joined[:, width:2 * width].reshape(LENGTH, heads, head_dim), cosine, sine).astype(jnp.bfloat16)
    v_half = joined[:, 2 * width:].reshape(LENGTH, heads, head_dim).astype(jnp.bfloat16)
    key_pad = jnp.pad(k_rot, ((half, half), (0, 0), (0, 0)))
    value_pad = jnp.pad(v_half, ((half, half), (0, 0), (0, 0)))

    def forward_block(block_index):
        scores, query_blk, key_blk = block_scores(block_index, q_rot, key_pad, qblock, half)
        row_max = lax.optimization_barrier(jnp.max(scores, axis=-1, keepdims=True))
        log_total = row_max + jnp.log(lax.optimization_barrier(jnp.sum(jnp.exp(scores - row_max), axis=-1, keepdims=True)))
        probs_half = jnp.exp(scores - log_total).astype(jnp.bfloat16)
        value_blk = lax.dynamic_slice_in_dim(value_pad, block_index * qblock, qblock + 2 * half, 0)
        output_blk = jnp.einsum('hqk,khd->qhd', probs_half.astype(jnp.float32), value_blk.astype(jnp.float32))
        return (output_blk.astype(jnp.bfloat16), log_total)
    block_ids = jnp.arange(blocks_count, dtype=jnp.int32)
    outputs, log_totals = lax.map(forward_block, block_ids)
    attended = outputs.reshape(LENGTH, width)
    resid = source32 + jnp.dot(attended, w_output, preferred_element_type=jnp.float32)
    normed_g, norm_two, inv_two = norm_apply(resid, gain_two)
    normed_two = normed_g.astype(jnp.bfloat16)
    expanded = jnp.dot(normed_two, w_expand, preferred_element_type=jnp.float32)
    pre_act = expanded[:, :FF]
    gate_part = expanded[:, FF:]
    activated = jax.nn.gelu(pre_act, approximate=False)
    mixed = (activated * gate_part).astype(jnp.bfloat16)
    layer_out = (resid + jnp.dot(mixed, w_contract, preferred_element_type=jnp.float32)).astype(jnp.bfloat16)
    contract_grad = jnp.dot(mixed.T, upstream_half, preferred_element_type=jnp.float32)
    d_mixed = jnp.dot(upstream_half, w_contract.T, preferred_element_type=jnp.float32)
    d_expanded = jnp.concatenate([d_mixed * gate_part * gelu_slope(pre_act), d_mixed * activated], axis=-1).astype(jnp.bfloat16)
    expand_grad = jnp.dot(normed_two.T, d_expanded, preferred_element_type=jnp.float32)
    d_normed_two = jnp.dot(d_expanded, w_expand.T, preferred_element_type=jnp.float32)
    d_resid_n, gain_two_grad = norm_back(d_normed_two, norm_two, inv_two, gain_two)
    d_resid = upstream + d_resid_n
    d_resid_half = d_resid.astype(jnp.bfloat16)
    output_grad = jnp.dot(attended.T, d_resid_half, preferred_element_type=jnp.float32)
    d_attended = jnp.dot(d_resid_half, w_output.T, preferred_element_type=jnp.float32).astype(jnp.bfloat16)
    d_attended = d_attended.reshape(LENGTH, heads, head_dim)

    def backward_block(block_index):
        scores, query_blk, key_blk = block_scores(block_index, q_rot, key_pad, qblock, half)
        log_total = log_totals[block_index]
        probs = jnp.exp(scores - log_total)
        probs_half = probs.astype(jnp.bfloat16).astype(jnp.float32)
        value_blk = lax.dynamic_slice_in_dim(value_pad, block_index * qblock, qblock + 2 * half, 0).astype(jnp.float32)
        d_out_blk = lax.dynamic_slice_in_dim(d_attended, block_index * qblock, qblock, 0).astype(jnp.float32)
        d_probs = jnp.einsum('qhd,khd->hqk', d_out_blk, value_blk)
        centred = d_probs - lax.optimization_barrier(jnp.sum(probs * d_probs, axis=-1, keepdims=True))
        d_scores = (probs * centred * head_dim ** (-0.5)).astype(jnp.bfloat16).astype(jnp.float32)
        d_query = jnp.einsum('hqk,khd->qhd', d_scores, key_blk)
        d_key = jnp.einsum('hqk,qhd->khd', d_scores, query_blk)
        d_value = jnp.einsum('hqk,qhd->khd', probs_half, d_out_blk)
        return (d_query, d_key, d_value)
    d_queries, d_key_blocks, d_value_blocks = lax.map(backward_block, block_ids)
    d_query = d_queries.reshape(LENGTH, heads, head_dim)
    d_key = spread_keys(d_key_blocks, half, qblock)
    d_value = spread_keys(d_value_blocks, half, qblock)
    d_joined = jnp.concatenate([unrotate(d_query, cosine, sine).reshape(LENGTH, width), unrotate(d_key, cosine, sine).reshape(LENGTH, width), d_value.reshape(LENGTH, width)], axis=-1).astype(jnp.bfloat16)
    joined_grad = jnp.dot(normed_one.T, d_joined, preferred_element_type=jnp.float32)
    d_normed_one = jnp.dot(d_joined, w_joined.T, preferred_element_type=jnp.float32)
    d_source, gain_one_grad = norm_back(d_normed_one, norm_one, inv_one, gain_one)
    input_grad = (d_resid + d_source).astype(jnp.bfloat16)
    grads = (joined_grad, output_grad, expand_grad, contract_grad, gain_one_grad, gain_two_grad)
    return (layer_out, input_grad, grads)

def reference(layer_input, cotangent, w_joined, w_output, w_expand, w_contract, gain_one, gain_two):
    weights = (w_joined, w_output, w_expand, w_contract, gain_one, gain_two)
    sources = layer_input.reshape(MB * BATCH, LENGTH, D)
    upstreams = cotangent.reshape(MB * BATCH, LENGTH, D)
    start = tuple((jnp.zeros(w.shape, jnp.float32) for w in weights))

    def step(carry, pair):
        layer_out, input_grad, grads = one_sequence(pair[0], pair[1], weights)
        return (tuple((c + g for c, g in zip(carry, grads))), (layer_out, input_grad))
    totals, (outputs, input_grads) = lax.scan(step, start, (sources, upstreams))
    return (outputs.reshape(MB, BATCH, LENGTH, D), input_grads.reshape(MB, BATCH, LENGTH, D), totals[0], totals[1], totals[2], totals[3], totals[4], totals[5])
```

```python
import jax
import jax.numpy as jnp
from jax import lax
from jax.sharding import PartitionSpec as P

HEADS = 12
HEAD_DIM = 64
WINDOW = 128


NORM_EPS = 1e-05
ROPE_BASE = 10000.0
MASK_FILL = -1e30
SQRT_HALF = 0.7071067811865476
INV_ROOT_TAU = 0.3989422804014327


LANES = 128


def scatter_sum(value, axes):
    value = value.astype(jnp.bfloat16)
    for axis in axes:
        size = lax.axis_size(axis)
        blocks = value.reshape(size, value.shape[0] // size, value.shape[1])
        value = jnp.sum(lax.all_to_all(blocks, axis, 0, 0).astype(jnp.float32), axis=0)
    return value


def norm_apply(values, gain):
    center = jnp.mean(values, axis=-1, keepdims=True)
    shifted = values - center
    inv_std = lax.rsqrt(jnp.mean(shifted * shifted, axis=-1, keepdims=True) + NORM_EPS)
    normed = shifted * inv_std
    return (normed * gain.astype(jnp.float32), normed, inv_std)


def norm_back(upstream, normed, inv_std, gain):
    scaled = upstream * gain.astype(jnp.float32)
    inner = (
        scaled
        - jnp.mean(scaled, axis=-1, keepdims=True)
        - normed * jnp.mean(scaled * normed, axis=-1, keepdims=True)
    )
    return (inv_std * inner, jnp.sum(upstream * normed, axis=(0, 1)))


def gelu_slope(values):
    cumul = 0.5 * (1.0 + jax.scipy.special.erf(values * SQRT_HALF))
    return cumul + values * jnp.exp(-0.5 * values * values) * INV_ROOT_TAU


def rope_tables(positions, head_dim):
    half_dim = head_dim // 2
    freqs = ROPE_BASE ** (-jnp.arange(half_dim).astype(jnp.float32) * 2.0 / head_dim)
    angles = positions.astype(jnp.float32)[:, None] * freqs[None, :]
    return (jnp.cos(angles)[:, None, :], jnp.sin(angles)[:, None, :])


def rotate(values, cosine, sine):
    half_dim = values.shape[-1] // 2
    first = values[..., :half_dim]
    second = values[..., half_dim:]
    return jnp.concatenate(
        [first * cosine - second * sine, second * cosine + first * sine], axis=-1
    )


def unrotate(values, cosine, sine):
    half_dim = values.shape[-1] // 2
    first = values[..., :half_dim]
    second = values[..., half_dim:]
    return jnp.concatenate(
        [first * cosine + second * sine, second * cosine - first * sine], axis=-1
    )


def per_device(
    layer_input, cotangent, w_joined, w_output, w_expand, w_contract, gain_one, gain_two
):
    micro, local_batch, group, width = layer_input.shape
    heads = HEADS
    head_dim = HEAD_DIM
    half = WINDOW // 2
    ffn = w_contract.shape[0]
    batch = micro * local_batch
    scale = head_dim ** (-0.5)
    axes = ("dp", "seq")
    seq_count = lax.axis_size("seq")
    up = [(i, i + 1) for i in range(seq_count - 1)]
    down = [(j, i) for i, j in up]
    group_start = lax.axis_index("seq") * group
    cosine, sine = rope_tables(group_start + jnp.arange(group, dtype=jnp.int32), head_dim)
    query_pos = group_start + jnp.arange(group, dtype=jnp.int32)[:, None]
    key_pos = group_start - half + jnp.arange(group + 2 * half, dtype=jnp.int32)[None, :]
    allowed = (
        (jnp.abs(query_pos - key_pos) <= half) & (key_pos >= 0) & (key_pos < group * seq_count)
    )
    gains = jnp.pad(jnp.stack([gain_one, gain_two], axis=1), ((0, 0), (0, LANES - 2)))
    pack_one = jnp.concatenate([w_joined, gains], axis=1)
    pack_two = jnp.concatenate([w_expand, w_contract.T, w_output], axis=1)
    full_one = lax.all_gather(pack_one, axes, axis=0, tiled=True)
    full_two = lax.all_gather(pack_two, axes, axis=0, tiled=True)
    full_joined = full_one[:, : 3 * width]
    full_gain_one = full_one[:, 3 * width]
    full_gain_two = full_one[:, 3 * width + 1]
    full_expand = full_two[:, : 2 * ffn]
    full_contract = full_two[:, 2 * ffn : 3 * ffn]
    full_output = full_two[:, 3 * ffn :]

    source32 = layer_input.reshape(batch, group, width).astype(jnp.float32)
    upstream_half = cotangent.reshape(batch, group, width)
    normed_f, norm_one, inv_one = norm_apply(source32, full_gain_one)
    normed_one = normed_f.astype(jnp.bfloat16)
    joined = jnp.einsum(
        "bcd,de->bce", normed_one, full_joined, preferred_element_type=jnp.float32
    )
    shape_heads = (batch, group, heads, head_dim)
    k_rot = rotate(joined[..., width : 2 * width].reshape(shape_heads), cosine, sine).astype(
        jnp.bfloat16
    )
    v_half = joined[..., 2 * width :].astype(jnp.bfloat16)
    key_value = jnp.stack([k_rot.reshape(batch, group, width), v_half])
    before = lax.ppermute(key_value[:, :, group - half :], "seq", up)
    after = lax.ppermute(key_value[:, :, :half], "seq", down)
    q_rot = rotate(joined[..., :width].reshape(shape_heads), cosine, sine).astype(jnp.bfloat16)
    extended = jnp.concatenate([before, key_value, after], axis=2)
    ext_shape = (batch, group + 2 * half, heads, head_dim)
    key_rows = extended[0].reshape(ext_shape)
    value_rows = extended[1].reshape(ext_shape)
    scores = (
        jnp.einsum("bqhd,bkhd->bhqk", q_rot, key_rows, preferred_element_type=jnp.float32)
        * scale
    )
    scores = jnp.where(allowed[None, None], scores, MASK_FILL)
    row_max = jnp.max(scores, axis=-1, keepdims=True)
    log_total = row_max + jnp.log(jnp.sum(jnp.exp(scores - row_max), axis=-1, keepdims=True))
    probs = jnp.exp(scores - log_total)
    probs_half = probs.astype(jnp.bfloat16)
    attended = jnp.einsum(
        "bhqk,bkhd->bqhd", probs_half, value_rows, preferred_element_type=jnp.float32
    )
    attended = attended.astype(jnp.bfloat16).reshape(batch, group, width)
    resid = source32 + jnp.einsum(
        "bcd,de->bce", attended, full_output, preferred_element_type=jnp.float32
    )
    normed_g, norm_two, inv_two = norm_apply(resid, full_gain_two)
    normed_two = normed_g.astype(jnp.bfloat16)
    expanded = jnp.einsum(
        "bcd,de->bce", normed_two, full_expand, preferred_element_type=jnp.float32
    )
    pre_act = expanded[..., :ffn]
    gate_part = expanded[..., ffn:]
    activated = jax.nn.gelu(pre_act, approximate=False)
    mixed = (activated * gate_part).astype(jnp.bfloat16)
    contract_acc = jnp.einsum(
        "bcd,bcf->df", upstream_half, mixed, preferred_element_type=jnp.float32
    )
    d_mixed = jnp.einsum(
        "bcd,df->bcf", upstream_half, full_contract, preferred_element_type=jnp.float32
    )
    d_expanded = jnp.concatenate(
        [d_mixed * gate_part * gelu_slope(pre_act), d_mixed * activated], axis=-1
    ).astype(jnp.bfloat16)
    expand_acc = jnp.einsum(
        "bcd,bce->de", normed_two, d_expanded, preferred_element_type=jnp.float32
    )
    ffn_sum = scatter_sum(jnp.concatenate([expand_acc, contract_acc], axis=1), axes)
    d_normed_two = jnp.einsum(
        "bce,de->bcd", d_expanded, full_expand, preferred_element_type=jnp.float32
    )
    d_resid_n, gain_two_part = norm_back(d_normed_two, norm_two, inv_two, full_gain_two)
    d_resid = upstream_half.astype(jnp.float32) + d_resid_n
    d_resid_half = d_resid.astype(jnp.bfloat16)
    d_attended = jnp.einsum(
        "bce,de->bcd", d_resid_half, full_output, preferred_element_type=jnp.float32
    )
    d_attended = d_attended.astype(jnp.bfloat16).reshape(shape_heads)
    d_probs = jnp.einsum(
        "bqhd,bkhd->bhqk", d_attended, value_rows, preferred_element_type=jnp.float32
    )
    centred = d_probs - jnp.sum(probs * d_probs, axis=-1, keepdims=True)
    d_scores = (probs * centred * scale).astype(jnp.bfloat16)
    d_key_ext = jnp.einsum(
        "bhqk,bqhd->bkhd", d_scores, q_rot, preferred_element_type=jnp.float32
    )
    d_value_ext = jnp.einsum(
        "bhqk,bqhd->bkhd", probs_half, d_attended, preferred_element_type=jnp.float32
    )
    ext_grads = jnp.stack(
        [
            d_key_ext.reshape(batch, group + 2 * half, width),
            d_value_ext.reshape(batch, group + 2 * half, width),
        ]
    )
    rims = ext_grads.astype(jnp.bfloat16)
    from_left = lax.ppermute(rims[:, :, group + half :], "seq", up).astype(jnp.float32)
    from_right = lax.ppermute(rims[:, :, :half], "seq", down).astype(jnp.float32)
    d_query = jnp.einsum(
        "bhqk,bkhd->bqhd", d_scores, key_rows, preferred_element_type=jnp.float32
    )
    output_acc = jnp.einsum(
        "bcd,bce->de", attended, d_resid_half, preferred_element_type=jnp.float32
    )
    final = resid + jnp.einsum(
        "bcf,df->bcd", mixed, full_contract, preferred_element_type=jnp.float32
    )
    own_grads = ext_grads[:, :, half : half + group]
    own_grads = own_grads + jnp.pad(
        from_left, ((0, 0), (0, 0), (0, group - half), (0, 0))
    ) + jnp.pad(from_right, ((0, 0), (0, 0), (group - half, 0), (0, 0)))
    d_key = unrotate(own_grads[0].reshape(shape_heads), cosine, sine).reshape(
        batch, group, width
    )
    d_query_flat = unrotate(d_query, cosine, sine).reshape(batch, group, width)
    d_joined = jnp.concatenate([d_query_flat, d_key, own_grads[1]], axis=-1).astype(
        jnp.bfloat16
    )
    d_normed_one = jnp.einsum(
        "bce,de->bcd", d_joined, full_joined, preferred_element_type=jnp.float32
    )
    d_source, gain_one_part = norm_back(d_normed_one, norm_one, inv_one, full_gain_one)
    input_grad = (d_resid + d_source).astype(jnp.bfloat16)
    joined_acc = jnp.einsum(
        "bcd,bce->de", normed_one, d_joined, preferred_element_type=jnp.float32
    )
    gain_parts = jnp.pad(
        jnp.stack([gain_one_part, gain_two_part], axis=1), ((0, 0), (0, LANES - 2))
    )
    last_sum = scatter_sum(jnp.concatenate([joined_acc, output_acc, gain_parts], axis=1), axes)
    return (
        final.astype(jnp.bfloat16).reshape(layer_input.shape),
        input_grad.reshape(layer_input.shape),
        last_sum[:, : 3 * width],
        last_sum[:, 3 * width : 4 * width],
        ffn_sum[:, : 2 * ffn],
        ffn_sum[:, 2 * ffn :].T,
        last_sum[:, 4 * width],
        last_sum[:, 4 * width + 1],
    )


def solution(mesh):
    placed = (
        P(None, "dp", "seq", None),
        P(None, "dp", "seq", None),
        P(("dp", "seq"), None),
        P(("dp", "seq"), None),
        P(("dp", "seq"), None),
        P(None, ("dp", "seq")),
        P(("dp", "seq")),
        P(("dp", "seq")),
    )
    return jax.shard_map(
        per_device,
        mesh=mesh,
        in_specs=placed,
        out_specs=(
            P(None, "dp", "seq", None),
            P(None, "dp", "seq", None),
            P(("dp", "seq"), None),
            P(("dp", "seq"), None),
            P(("dp", "seq"), None),
            P(None, ("dp", "seq")),
            P(("dp", "seq")),
            P(("dp", "seq")),
        ),
        check_vma=False,
    )
```

```python
import jax
import jax.numpy as jnp
from jax import lax
from jax.sharding import PartitionSpec as P

HEADS = 12
HEAD_DIM = 64
WINDOW = 128


NORM_EPS = 1e-05
ROPE_BASE = 10000.0
MASK_FILL = -1e30
SQRT_HALF = 0.7071067811865476
INV_ROOT_TAU = 0.3989422804014327


LANES = 128


def scatter_sum(value, axes):
    outer, inner = axes
    outer_size, inner_size = (lax.axis_size(outer), lax.axis_size(inner))
    pairs = outer_size // 2
    place = lax.axis_index(outer)
    core = place % 2
    blocks = value.reshape(pairs, 2, value.shape[0] // outer_size, value.shape[1])
    other = lax.dynamic_index_in_dim(blocks, 1 - core, axis=1, keepdims=False)
    own = lax.dynamic_index_in_dim(blocks, core, axis=1, keepdims=False)
    swap = [(i, i ^ 1) for i in range(outer_size)]
    value = own + lax.ppermute(other, outer, swap)
    if pairs == 2:
        line = place // 2
        other = lax.dynamic_index_in_dim(value, 1 - line, axis=0, keepdims=False)
        own = lax.dynamic_index_in_dim(value, line, axis=0, keepdims=False)
        swap = [(i, i ^ 2) for i in range(outer_size)]
        arrived = lax.ppermute(other.astype(jnp.bfloat16), outer, swap)
        value = own + arrived.astype(jnp.float32)
    else:
        groups = [list(range(c, outer_size, 2)) for c in range(2)]
        arrived = lax.all_to_all(
            value.astype(jnp.bfloat16), outer, 0, 0, axis_index_groups=groups
        )
        value = jnp.sum(arrived.astype(jnp.float32), axis=0)
    blocks = value.reshape(inner_size, value.shape[0] // inner_size, value.shape[1])
    return jnp.sum(lax.all_to_all(blocks, inner, 0, 0), axis=0)


def norm_apply(values, gain):
    center = jnp.mean(values, axis=-1, keepdims=True)
    shifted = values - center
    inv_std = lax.rsqrt(jnp.mean(shifted * shifted, axis=-1, keepdims=True) + NORM_EPS)
    normed = shifted * inv_std
    return (normed * gain.astype(jnp.float32), normed, inv_std)


def norm_back(upstream, normed, inv_std, gain):
    scaled = upstream * gain.astype(jnp.float32)
    inner = (
        scaled
        - jnp.mean(scaled, axis=-1, keepdims=True)
        - normed * jnp.mean(scaled * normed, axis=-1, keepdims=True)
    )
    return (inv_std * inner, jnp.sum(upstream * normed, axis=(0, 1)))


def gelu_slope(values):
    cumul = 0.5 * (1.0 + jax.scipy.special.erf(values * SQRT_HALF))
    return cumul + values * jnp.exp(-0.5 * values * values) * INV_ROOT_TAU


def rope_tables(positions, head_dim):
    half_dim = head_dim // 2
    freqs = ROPE_BASE ** (-jnp.arange(half_dim).astype(jnp.float32) * 2.0 / head_dim)
    angles = positions.astype(jnp.float32)[:, None] * freqs[None, :]
    return (jnp.cos(angles)[:, None, :], jnp.sin(angles)[:, None, :])


def rotate(values, cosine, sine):
    half_dim = values.shape[-1] // 2
    first = values[..., :half_dim]
    second = values[..., half_dim:]
    return jnp.concatenate(
        [first * cosine - second * sine, second * cosine + first * sine], axis=-1
    )


def unrotate(values, cosine, sine):
    half_dim = values.shape[-1] // 2
    first = values[..., :half_dim]
    second = values[..., half_dim:]
    return jnp.concatenate(
        [first * cosine + second * sine, second * cosine - first * sine], axis=-1
    )


def per_device(
    layer_input, cotangent, w_joined, w_output, w_expand, w_contract, gain_one, gain_two
):
    micro, local_batch, group, width = layer_input.shape
    heads = HEADS
    head_dim = HEAD_DIM
    half = WINDOW // 2
    ffn = w_contract.shape[0]
    batch = micro * local_batch
    scale = head_dim ** (-0.5)
    axes = ("dp", "seq")
    seq_count = lax.axis_size("seq")
    up = [(i, i + 1) for i in range(seq_count - 1)]
    down = [(j, i) for i, j in up]
    group_start = lax.axis_index("seq") * group
    cosine, sine = rope_tables(group_start + jnp.arange(group, dtype=jnp.int32), head_dim)
    query_pos = group_start + jnp.arange(group, dtype=jnp.int32)[:, None]
    key_pos = group_start - half + jnp.arange(group + 2 * half, dtype=jnp.int32)[None, :]
    allowed = (
        (jnp.abs(query_pos - key_pos) <= half) & (key_pos >= 0) & (key_pos < group * seq_count)
    )
    gains = jnp.pad(jnp.stack([gain_one, gain_two], axis=1), ((0, 0), (0, LANES - 2)))
    pack_one = jnp.concatenate([w_joined, gains], axis=1)
    pack_two = jnp.concatenate([w_expand, w_contract.T, w_output], axis=1)
    full_one = lax.all_gather(pack_one, axes, axis=0, tiled=True)
    full_two = lax.all_gather(pack_two, axes, axis=0, tiled=True)
    full_joined = full_one[:, : 3 * width]
    full_gain_one = full_one[:, 3 * width]
    full_gain_two = full_one[:, 3 * width + 1]
    full_expand = full_two[:, : 2 * ffn]
    full_contract = full_two[:, 2 * ffn : 3 * ffn]
    full_output = full_two[:, 3 * ffn :]

    source32 = layer_input.reshape(batch, group, width).astype(jnp.float32)
    upstream_half = cotangent.reshape(batch, group, width)
    normed_f, norm_one, inv_one = norm_apply(source32, full_gain_one)
    normed_one = normed_f.astype(jnp.bfloat16)
    joined = jnp.einsum(
        "bcd,de->bce", normed_one, full_joined, preferred_element_type=jnp.float32
    )
    shape_heads = (batch, group, heads, head_dim)
    k_rot = rotate(joined[..., width : 2 * width].reshape(shape_heads), cosine, sine).astype(
        jnp.bfloat16
    )
    v_half = joined[..., 2 * width :].astype(jnp.bfloat16)
    key_value = jnp.stack([k_rot.reshape(batch, group, width), v_half])
    before = lax.ppermute(key_value[:, :, group - half :], "seq", up)
    after = lax.ppermute(key_value[:, :, :half], "seq", down)
    q_rot = rotate(joined[..., :width].reshape(shape_heads), cosine, sine).astype(jnp.bfloat16)
    extended = jnp.concatenate([before, key_value, after], axis=2)
    ext_shape = (batch, group + 2 * half, heads, head_dim)
    key_rows = extended[0].reshape(ext_shape)
    value_rows = extended[1].reshape(ext_shape)
    scores = (
        jnp.einsum("bqhd,bkhd->bhqk", q_rot, key_rows, preferred_element_type=jnp.float32)
        * scale
    )
    scores = jnp.where(allowed[None, None], scores, MASK_FILL)
    row_max = jnp.max(scores, axis=-1, keepdims=True)
    log_total = row_max + jnp.log(jnp.sum(jnp.exp(scores - row_max), axis=-1, keepdims=True))
    probs = jnp.exp(scores - log_total)
    probs_half = probs.astype(jnp.bfloat16)
    attended = jnp.einsum(
        "bhqk,bkhd->bqhd", probs_half, value_rows, preferred_element_type=jnp.float32
    )
    attended = attended.astype(jnp.bfloat16).reshape(batch, group, width)
    resid = source32 + jnp.einsum(
        "bcd,de->bce", attended, full_output, preferred_element_type=jnp.float32
    )
    normed_g, norm_two, inv_two = norm_apply(resid, full_gain_two)
    normed_two = normed_g.astype(jnp.bfloat16)
    expanded = jnp.einsum(
        "bcd,de->bce", normed_two, full_expand, preferred_element_type=jnp.float32
    )
    pre_act = expanded[..., :ffn]
    gate_part = expanded[..., ffn:]
    activated = jax.nn.gelu(pre_act, approximate=False)
    mixed = (activated * gate_part).astype(jnp.bfloat16)
    contract_acc = jnp.einsum(
        "bcd,bcf->df", upstream_half, mixed, preferred_element_type=jnp.float32
    )
    d_mixed = jnp.einsum(
        "bcd,df->bcf", upstream_half, full_contract, preferred_element_type=jnp.float32
    )
    d_expanded = jnp.concatenate(
        [d_mixed * gate_part * gelu_slope(pre_act), d_mixed * activated], axis=-1
    ).astype(jnp.bfloat16)
    expand_acc = jnp.einsum(
        "bcd,bce->de", normed_two, d_expanded, preferred_element_type=jnp.float32
    )
    ffn_grads, d_expanded = lax.optimization_barrier(
        (jnp.concatenate([expand_acc, contract_acc], axis=1), d_expanded)
    )
    ffn_sum = scatter_sum(ffn_grads, axes)
    d_normed_two = jnp.einsum(
        "bce,de->bcd", d_expanded, full_expand, preferred_element_type=jnp.float32
    )
    d_resid_n, gain_two_part = norm_back(d_normed_two, norm_two, inv_two, full_gain_two)
    d_resid = upstream_half.astype(jnp.float32) + d_resid_n
    d_resid_half = d_resid.astype(jnp.bfloat16)
    d_attended = jnp.einsum(
        "bce,de->bcd", d_resid_half, full_output, preferred_element_type=jnp.float32
    )
    d_attended = d_attended.astype(jnp.bfloat16).reshape(shape_heads)
    d_probs = jnp.einsum(
        "bqhd,bkhd->bhqk", d_attended, value_rows, preferred_element_type=jnp.float32
    )
    centred = d_probs - jnp.sum(probs * d_probs, axis=-1, keepdims=True)
    d_scores = (probs * centred * scale).astype(jnp.bfloat16)
    d_key_ext = jnp.einsum(
        "bhqk,bqhd->bkhd", d_scores, q_rot, preferred_element_type=jnp.float32
    )
    d_value_ext = jnp.einsum(
        "bhqk,bqhd->bkhd", probs_half, d_attended, preferred_element_type=jnp.float32
    )
    ext_grads = jnp.stack(
        [
            d_key_ext.reshape(batch, group + 2 * half, width),
            d_value_ext.reshape(batch, group + 2 * half, width),
        ]
    )
    rims = ext_grads.astype(jnp.bfloat16)
    from_left = lax.ppermute(rims[:, :, group + half :], "seq", up).astype(jnp.float32)
    from_right = lax.ppermute(rims[:, :, :half], "seq", down).astype(jnp.float32)
    d_query = jnp.einsum(
        "bhqk,bkhd->bqhd", d_scores, key_rows, preferred_element_type=jnp.float32
    )
    output_acc = jnp.einsum(
        "bcd,bce->de", attended, d_resid_half, preferred_element_type=jnp.float32
    )
    final = resid + jnp.einsum(
        "bcf,df->bcd", mixed, full_contract, preferred_element_type=jnp.float32
    )
    own_grads = ext_grads[:, :, half : half + group]
    own_grads = own_grads + jnp.pad(
        from_left, ((0, 0), (0, 0), (0, group - half), (0, 0))
    ) + jnp.pad(from_right, ((0, 0), (0, 0), (group - half, 0), (0, 0)))
    d_key = unrotate(own_grads[0].reshape(shape_heads), cosine, sine).reshape(
        batch, group, width
    )
    d_query_flat = unrotate(d_query, cosine, sine).reshape(batch, group, width)
    d_joined = jnp.concatenate([d_query_flat, d_key, own_grads[1]], axis=-1).astype(
        jnp.bfloat16
    )
    d_normed_one = jnp.einsum(
        "bce,de->bcd", d_joined, full_joined, preferred_element_type=jnp.float32
    )
    d_source, gain_one_part = norm_back(d_normed_one, norm_one, inv_one, full_gain_one)
    input_grad = (d_resid + d_source).astype(jnp.bfloat16)
    joined_acc = jnp.einsum(
        "bcd,bce->de", normed_one, d_joined, preferred_element_type=jnp.float32
    )
    gain_parts = jnp.pad(
        jnp.stack([gain_one_part, gain_two_part], axis=1), ((0, 0), (0, LANES - 2))
    )
    last_sum = scatter_sum(jnp.concatenate([joined_acc, output_acc, gain_parts], axis=1), axes)
    return (
        final.astype(jnp.bfloat16).reshape(layer_input.shape),
        input_grad.reshape(layer_input.shape),
        last_sum[:, : 3 * width],
        last_sum[:, 3 * width : 4 * width],
        ffn_sum[:, : 2 * ffn],
        ffn_sum[:, 2 * ffn :].T,
        last_sum[:, 4 * width],
        last_sum[:, 4 * width + 1],
    )


def solution(mesh):
    placed = (
        P(None, "dp", "seq", None),
        P(None, "dp", "seq", None),
        P(("dp", "seq"), None),
        P(("dp", "seq"), None),
        P(("dp", "seq"), None),
        P(None, ("dp", "seq")),
        P(("dp", "seq")),
        P(("dp", "seq")),
    )
    return jax.shard_map(
        per_device,
        mesh=mesh,
        in_specs=placed,
        out_specs=(
            P(None, "dp", "seq", None),
            P(None, "dp", "seq", None),
            P(("dp", "seq"), None),
            P(("dp", "seq"), None),
            P(("dp", "seq"), None),
            P(None, ("dp", "seq")),
            P(("dp", "seq")),
            P(("dp", "seq")),
        ),
        check_vma=False,
    )
```

```python
import jax
import jax.numpy as jnp
from jax import lax
from jax.sharding import PartitionSpec as P

HEADS = 12
HEAD_DIM = 64
WINDOW = 128


NORM_EPS = 1e-05
ROPE_BASE = 10000.0
MASK_FILL = -1e30
SQRT_HALF = 0.7071067811865476
INV_ROOT_TAU = 0.3989422804014327


LANES = 128


def pair_sum(value, outer):
    outer_size = lax.axis_size(outer)
    pairs = outer_size // 2
    core = lax.axis_index(outer) % 2
    blocks = value.reshape(pairs, 2, value.shape[0] // outer_size, value.shape[1])
    other = lax.dynamic_index_in_dim(blocks, 1 - core, axis=1, keepdims=False)
    own = lax.dynamic_index_in_dim(blocks, core, axis=1, keepdims=False)
    swap = [(i, i ^ 1) for i in range(outer_size)]
    return own + lax.ppermute(other, outer, swap)


def line_sum(value, outer):
    outer_size = lax.axis_size(outer)
    if outer_size == 4:
        line = lax.axis_index(outer) // 2
        other = lax.dynamic_index_in_dim(value, 1 - line, axis=0, keepdims=False)
        own = lax.dynamic_index_in_dim(value, line, axis=0, keepdims=False)
        swap = [(i, i ^ 2) for i in range(outer_size)]
        arrived = lax.ppermute(other.astype(jnp.bfloat16), outer, swap)
        value = own + arrived.astype(jnp.float32)
    else:
        groups = [list(range(c, outer_size, 2)) for c in range(2)]
        arrived = lax.all_to_all(
            value.astype(jnp.bfloat16), outer, 0, 0, axis_index_groups=groups
        )
        value = jnp.sum(arrived.astype(jnp.float32), axis=0)
    return value


def ring_sum(value, inner):
    inner_size = lax.axis_size(inner)
    blocks = value.reshape(inner_size, value.shape[0] // inner_size, value.shape[1])
    return jnp.sum(lax.all_to_all(blocks, inner, 0, 0), axis=0)


def norm_apply(values, gain):
    center = jnp.mean(values, axis=-1, keepdims=True)
    shifted = values - center
    inv_std = lax.rsqrt(jnp.mean(shifted * shifted, axis=-1, keepdims=True) + NORM_EPS)
    normed = shifted * inv_std
    return (normed * gain.astype(jnp.float32), normed, inv_std)


def norm_back(upstream, normed, inv_std, gain):
    scaled = upstream * gain.astype(jnp.float32)
    inner = (
        scaled
        - jnp.mean(scaled, axis=-1, keepdims=True)
        - normed * jnp.mean(scaled * normed, axis=-1, keepdims=True)
    )
    return (inv_std * inner, jnp.sum(upstream * normed, axis=(0, 1)))


def gelu_slope(values):
    cumul = 0.5 * (1.0 + jax.scipy.special.erf(values * SQRT_HALF))
    return cumul + values * jnp.exp(-0.5 * values * values) * INV_ROOT_TAU


def rope_tables(positions, head_dim):
    half_dim = head_dim // 2
    freqs = ROPE_BASE ** (-jnp.arange(half_dim).astype(jnp.float32) * 2.0 / head_dim)
    angles = positions.astype(jnp.float32)[:, None] * freqs[None, :]
    return (jnp.cos(angles)[:, None, :], jnp.sin(angles)[:, None, :])


def rotate(values, cosine, sine):
    half_dim = values.shape[-1] // 2
    first = values[..., :half_dim]
    second = values[..., half_dim:]
    return jnp.concatenate(
        [first * cosine - second * sine, second * cosine + first * sine], axis=-1
    )


def unrotate(values, cosine, sine):
    half_dim = values.shape[-1] // 2
    first = values[..., :half_dim]
    second = values[..., half_dim:]
    return jnp.concatenate(
        [first * cosine + second * sine, second * cosine - first * sine], axis=-1
    )


def per_device(
    layer_input, cotangent, w_joined, w_output, w_expand, w_contract, gain_one, gain_two
):
    micro, local_batch, group, width = layer_input.shape
    heads = HEADS
    head_dim = HEAD_DIM
    half = WINDOW // 2
    ffn = w_contract.shape[0]
    batch = micro * local_batch
    scale = head_dim ** (-0.5)
    axes = ("dp", "seq")
    seq_count = lax.axis_size("seq")
    up = [(i, i + 1) for i in range(seq_count - 1)]
    down = [(j, i) for i, j in up]
    group_start = lax.axis_index("seq") * group
    cosine, sine = rope_tables(group_start + jnp.arange(group, dtype=jnp.int32), head_dim)
    query_pos = group_start + jnp.arange(group, dtype=jnp.int32)[:, None]
    key_pos = group_start - half + jnp.arange(group + 2 * half, dtype=jnp.int32)[None, :]
    allowed = (
        (jnp.abs(query_pos - key_pos) <= half) & (key_pos >= 0) & (key_pos < group * seq_count)
    )
    gains = jnp.pad(jnp.stack([gain_one, gain_two], axis=1), ((0, 0), (0, LANES - 2)))
    pack_one = jnp.concatenate([w_joined, gains], axis=1)
    pack_two = jnp.concatenate([w_expand, w_contract.T, w_output], axis=1)
    full_one = lax.all_gather(pack_one, axes, axis=0, tiled=True)
    full_two = lax.all_gather(pack_two, axes, axis=0, tiled=True)
    full_joined = full_one[:, : 3 * width]
    full_gain_one = full_one[:, 3 * width]
    full_gain_two = full_one[:, 3 * width + 1]
    full_expand = full_two[:, : 2 * ffn]
    full_contract = full_two[:, 2 * ffn : 3 * ffn]
    full_output = full_two[:, 3 * ffn :]

    source32 = layer_input.reshape(batch, group, width).astype(jnp.float32)
    upstream_half = cotangent.reshape(batch, group, width)
    normed_f, norm_one, inv_one = norm_apply(source32, full_gain_one)
    normed_one = normed_f.astype(jnp.bfloat16)
    joined = jnp.einsum(
        "bcd,de->bce", normed_one, full_joined, preferred_element_type=jnp.float32
    )
    shape_heads = (batch, group, heads, head_dim)
    k_rot = rotate(joined[..., width : 2 * width].reshape(shape_heads), cosine, sine).astype(
        jnp.bfloat16
    )
    v_half = joined[..., 2 * width :].astype(jnp.bfloat16)
    key_value = jnp.stack([k_rot.reshape(batch, group, width), v_half])
    before = lax.ppermute(key_value[:, :, group - half :], "seq", up)
    after = lax.ppermute(key_value[:, :, :half], "seq", down)
    q_rot = rotate(joined[..., :width].reshape(shape_heads), cosine, sine).astype(jnp.bfloat16)
    extended = jnp.concatenate([before, key_value, after], axis=2)
    ext_shape = (batch, group + 2 * half, heads, head_dim)
    key_rows = extended[0].reshape(ext_shape)
    value_rows = extended[1].reshape(ext_shape)
    scores = (
        jnp.einsum("bqhd,bkhd->bhqk", q_rot, key_rows, preferred_element_type=jnp.float32)
        * scale
    )
    scores = jnp.where(allowed[None, None], scores, MASK_FILL)
    row_max = jnp.max(scores, axis=-1, keepdims=True)
    log_total = row_max + jnp.log(jnp.sum(jnp.exp(scores - row_max), axis=-1, keepdims=True))
    probs = jnp.exp(scores - log_total)
    probs_half = probs.astype(jnp.bfloat16)
    attended = jnp.einsum(
        "bhqk,bkhd->bqhd", probs_half, value_rows, preferred_element_type=jnp.float32
    )
    attended = attended.astype(jnp.bfloat16).reshape(batch, group, width)
    resid = source32 + jnp.einsum(
        "bcd,de->bce", attended, full_output, preferred_element_type=jnp.float32
    )
    normed_g, norm_two, inv_two = norm_apply(resid, full_gain_two)
    normed_two = normed_g.astype(jnp.bfloat16)
    expanded = jnp.einsum(
        "bcd,de->bce", normed_two, full_expand, preferred_element_type=jnp.float32
    )
    pre_act = expanded[..., :ffn]
    gate_part = expanded[..., ffn:]
    activated = jax.nn.gelu(pre_act, approximate=False)
    mixed = (activated * gate_part).astype(jnp.bfloat16)
    contract_acc = jnp.einsum(
        "bcd,bcf->df", upstream_half, mixed, preferred_element_type=jnp.float32
    )
    d_mixed = jnp.einsum(
        "bcd,df->bcf", upstream_half, full_contract, preferred_element_type=jnp.float32
    )
    d_expanded = jnp.concatenate(
        [d_mixed * gate_part * gelu_slope(pre_act), d_mixed * activated], axis=-1
    ).astype(jnp.bfloat16)
    expand_acc = jnp.einsum(
        "bcd,bce->de", normed_two, d_expanded, preferred_element_type=jnp.float32
    )
    ffn_grads, d_expanded = lax.optimization_barrier(
        (jnp.concatenate([expand_acc, contract_acc], axis=1), d_expanded)
    )
    ffn_pair = pair_sum(ffn_grads, "dp")
    d_normed_two = jnp.einsum(
        "bce,de->bcd", d_expanded, full_expand, preferred_element_type=jnp.float32
    )
    d_resid_n, gain_two_part = norm_back(d_normed_two, norm_two, inv_two, full_gain_two)
    d_resid = upstream_half.astype(jnp.float32) + d_resid_n
    d_resid_half = d_resid.astype(jnp.bfloat16)
    ffn_pair, d_resid_half = lax.optimization_barrier((ffn_pair, d_resid_half))
    ffn_line = line_sum(ffn_pair, "dp")
    d_attended = jnp.einsum(
        "bce,de->bcd", d_resid_half, full_output, preferred_element_type=jnp.float32
    )
    d_attended = d_attended.astype(jnp.bfloat16).reshape(shape_heads)
    d_probs = jnp.einsum(
        "bqhd,bkhd->bhqk", d_attended, value_rows, preferred_element_type=jnp.float32
    )
    centred = d_probs - jnp.sum(probs * d_probs, axis=-1, keepdims=True)
    d_scores = (probs * centred * scale).astype(jnp.bfloat16)
    d_key_ext = jnp.einsum(
        "bhqk,bqhd->bkhd", d_scores, q_rot, preferred_element_type=jnp.float32
    )
    d_value_ext = jnp.einsum(
        "bhqk,bqhd->bkhd", probs_half, d_attended, preferred_element_type=jnp.float32
    )
    ext_grads = jnp.stack(
        [
            d_key_ext.reshape(batch, group + 2 * half, width),
            d_value_ext.reshape(batch, group + 2 * half, width),
        ]
    )
    rims = ext_grads.astype(jnp.bfloat16)
    ffn_line, rims = lax.optimization_barrier((ffn_line, rims))
    ffn_sum = ring_sum(ffn_line, "seq")
    from_left = lax.ppermute(rims[:, :, group + half :], "seq", up).astype(jnp.float32)
    from_right = lax.ppermute(rims[:, :, :half], "seq", down).astype(jnp.float32)
    d_query = jnp.einsum(
        "bhqk,bkhd->bqhd", d_scores, key_rows, preferred_element_type=jnp.float32
    )
    output_acc = jnp.einsum(
        "bcd,bce->de", attended, d_resid_half, preferred_element_type=jnp.float32
    )
    final = resid + jnp.einsum(
        "bcf,df->bcd", mixed, full_contract, preferred_element_type=jnp.float32
    )
    own_grads = ext_grads[:, :, half : half + group]
    own_grads = own_grads + jnp.pad(
        from_left, ((0, 0), (0, 0), (0, group - half), (0, 0))
    ) + jnp.pad(from_right, ((0, 0), (0, 0), (group - half, 0), (0, 0)))
    d_key = unrotate(own_grads[0].reshape(shape_heads), cosine, sine).reshape(
        batch, group, width
    )
    d_query_flat = unrotate(d_query, cosine, sine).reshape(batch, group, width)
    d_joined = jnp.concatenate([d_query_flat, d_key, own_grads[1]], axis=-1).astype(
        jnp.bfloat16
    )
    d_normed_one = jnp.einsum(
        "bce,de->bcd", d_joined, full_joined, preferred_element_type=jnp.float32
    )
    d_source, gain_one_part = norm_back(d_normed_one, norm_one, inv_one, full_gain_one)
    input_grad = (d_resid + d_source).astype(jnp.bfloat16)
    joined_acc = jnp.einsum(
        "bcd,bce->de", normed_one, d_joined, preferred_element_type=jnp.float32
    )
    gain_parts = jnp.pad(
        jnp.stack([gain_one_part, gain_two_part], axis=1), ((0, 0), (0, LANES - 2))
    )
    last_grads = jnp.concatenate([joined_acc, output_acc, gain_parts], axis=1)
    last_sum = ring_sum(line_sum(pair_sum(last_grads, "dp"), "dp"), "seq")
    return (
        final.astype(jnp.bfloat16).reshape(layer_input.shape),
        input_grad.reshape(layer_input.shape),
        last_sum[:, : 3 * width],
        last_sum[:, 3 * width : 4 * width],
        ffn_sum[:, : 2 * ffn],
        ffn_sum[:, 2 * ffn :].T,
        last_sum[:, 4 * width],
        last_sum[:, 4 * width + 1],
    )


def solution(mesh):
    placed = (
        P(None, "dp", "seq", None),
        P(None, "dp", "seq", None),
        P(("dp", "seq"), None),
        P(("dp", "seq"), None),
        P(("dp", "seq"), None),
        P(None, ("dp", "seq")),
        P(("dp", "seq")),
        P(("dp", "seq")),
    )
    return jax.shard_map(
        per_device,
        mesh=mesh,
        in_specs=placed,
        out_specs=(
            P(None, "dp", "seq", None),
            P(None, "dp", "seq", None),
            P(("dp", "seq"), None),
            P(("dp", "seq"), None),
            P(("dp", "seq"), None),
            P(None, ("dp", "seq")),
            P(("dp", "seq")),
            P(("dp", "seq")),
        ),
        check_vma=False,
    )
```
